32 devices in a mesh: angle: 2 (over core), tile: 4 (over y, x), cuts: 4 (over z).
Axes of the slice: x: 2, y: 2, z: 4, core: 2. Of those that a mesh axis runs over, the one named last changes fastest.
Arguments:
- objects: float32 [2, 2, 512, 512], P('angle', None, ('tile', 'cuts')), may hold values from -6 to 6
- illumination: float32 [2, 128, 128], replicated, may hold values from -6 to 6
- positions: int32 [2, 256, 2], P('angle', ('tile', 'cuts')), may hold values from 0 to 384
- amplitudes: bfloat16 [2, 256, 128, 128], P('angle', ('tile', 'cuts')), may hold values from 0.25 to 2.5
- projector: bfloat16 [1024, 4096], P(None, ('angle', 'cuts')), may hold values from -0.1875 to 0.1875
Outputs:
- new_objects: float32 [2, 2, 512, 512], P('angle', None, ('tile', 'cuts'))
- volume: float32 [512, 4096], P('tile', ('angle', 'cuts'))
The draws below stay inside these ranges and needn't reach their ends.
All inputs are finite; a program needn't handle non-finite values.
Results may differ from the reference program's by a relative error of at most 0.02.
Values may be sent and summed in bfloat16 or wider, within the bound.
No kernel may reach another device: no remote copies, remote signals or barrier semaphores. Data moves between devices by JAX's collectives and lax.ppermute only.
A program may use at most 64 MiB of HBM per device.

```python
import jax
import jax.numpy as jnp
from jax import lax

NPIX = 512
PSIZE = 128
PATCH_DEV = 16
ANGLES = 2
PATCHES = 256
VOXELS = 4096
N_TILE = 4
N_CUTS = 4


def plant(drawn, own_key, smallest, largest):
    longest = drawn.shape.index(max(drawn.shape))
    spots = []
    for shift in (0, 1):
        where = [jax.random.randint(jax.random.fold_in(own_key, axis), (), 0, length) for axis, length in enumerate(drawn.shape)]
        where[longest] = (where[longest] + shift) % drawn.shape[longest]
        spots.append(tuple(where))
    return drawn.at[spots[0]].set(smallest).at[spots[1]].set(largest)


def block_levels(rng, shape, split, smallest, high):
    def one(position, blocks):
        draws = jax.random.uniform(jax.random.fold_in(jax.random.fold_in(rng, 6), position), (blocks,), jnp.float32, smallest / len(split), high / len(split))
        return jnp.repeat(jnp.exp(draws), shape[position] // blocks).reshape((-1,) + (1,) * (len(shape) - position - 1))

    loudness = one(*split[0])
    for cut in split[1:]:
        loudness = loudness * one(*cut)
    return loudness


def scatter_about(own_key, shape, width, bound, shards=(), kind=jnp.bfloat16):
    drawn = jax.random.normal(own_key, shape, jnp.float32) * width
    if len(shards) > 0:
        drawn = block_levels(own_key, shape, shards, -0.22, 0.18) * drawn
    return jnp.clip(drawn, min=-bound, max=bound).astype(kind)


def setup_inputs(seed: int = 0) -> dict:
    key_list = jax.random.split(jax.random.key(seed), 6)
    objects = scatter_about(key_list[0], (ANGLES, 2, NPIX, NPIX), 1.0, 6.0, ((0, 2), (2, 16)), jnp.float32)
    illumination = scatter_about(key_list[1], (2, PSIZE, PSIZE), 1.0, 6.0, (), jnp.float32)
    positions = plant(jax.random.randint(key_list[2], (ANGLES, PATCHES, 2), 0, NPIX - PSIZE + 1), jax.random.fold_in(key_list[2], 1), 0, NPIX - PSIZE).astype(jnp.int32)
    amplitudes = jnp.clip(0.25 + 2.25 * jax.random.uniform(key_list[3], (ANGLES, PATCHES, PSIZE, PSIZE), jnp.float32) ** block_levels(key_list[3], (ANGLES, PATCHES, PSIZE, PSIZE), ((0, 2), (1, 16)), -0.2, 0.2), 0.25, 2.5).astype(jnp.bfloat16)
    projector = scatter_about(key_list[4], (ANGLES * NPIX, VOXELS), (ANGLES * NPIX) ** -0.5, 0.1875, ((1, 8),))
    return dict(objects=objects, illumination=illumination, positions=positions, amplitudes=amplitudes, projector=projector)


step_size = 0.1

def dft_tables(patch_width):
    grid_index = jnp.arange(patch_width, dtype=jnp.int32)
    product_mod = grid_index[:, None] * grid_index[None, :] % patch_width
    phase_table = product_mod.astype(jnp.float32) * (2.0 * jnp.pi / patch_width)
    norm_scale = 1.0 / jnp.sqrt(jnp.float32(patch_width))
    table_real = (jnp.cos(phase_table) * norm_scale).astype(jnp.bfloat16)
    table_imag = (-jnp.sin(phase_table) * norm_scale).astype(jnp.bfloat16)
    table_wide = jnp.concatenate([table_real, table_imag], axis=1)
    table_tall = jnp.concatenate([table_real, table_imag], axis=0)
    return (table_wide, table_tall)

def right_product(stacked, table_wide, conjugate):
    edge_width = stacked.shape[-1]
    result = jnp.einsum('ncij,jk->ncik', stacked.astype(jnp.float32), table_wide.astype(jnp.float32), precision=lax.Precision.HIGHEST)
    from_real = result[:, 0]
    from_imag = result[:, 1]
    if conjugate:
        real_part = from_real[..., :edge_width] + from_imag[..., edge_width:]
        imag_part = from_imag[..., :edge_width] - from_real[..., edge_width:]
    else:
        real_part = from_real[..., :edge_width] - from_imag[..., edge_width:]
        imag_part = from_imag[..., :edge_width] + from_real[..., edge_width:]
    return jnp.stack([real_part, imag_part], axis=1)

def left_product(table_tall, stacked, conjugate):
    edge_width = stacked.shape[-1]
    result = jnp.einsum('kj,ncjm->nckm', table_tall.astype(jnp.float32), stacked.astype(jnp.float32), precision=lax.Precision.HIGHEST)
    from_real = result[:, 0]
    from_imag = result[:, 1]
    if conjugate:
        real_part = from_real[:, :edge_width, :] + from_imag[:, edge_width:, :]
        imag_part = from_imag[:, :edge_width, :] - from_real[:, edge_width:, :]
    else:
        real_part = from_real[:, :edge_width, :] - from_imag[:, edge_width:, :]
        imag_part = from_imag[:, :edge_width, :] + from_real[:, edge_width:, :]
    return jnp.stack([real_part, imag_part], axis=1)

def patch_update(object_half, illumination, place_list, amp_block, table_wide, table_tall):
    edge_width = illumination.shape[-1]
    zero_index = jnp.zeros((), jnp.int32)

    def cut_window(row_at, col_at):
        return lax.dynamic_slice(object_half, (zero_index, row_at, col_at), (2, edge_width, edge_width))
    windows = jax.vmap(cut_window)(place_list[:, 0], place_list[:, 1]).astype(jnp.float32)
    probe_real = illumination[0]
    probe_imag = illumination[1]
    exit_real = probe_real * windows[:, 0] - probe_imag * windows[:, 1]
    exit_imag = probe_real * windows[:, 1] + probe_imag * windows[:, 0]
    exit_half = jnp.stack([exit_real, exit_imag], axis=1).astype(jnp.bfloat16)
    spread = right_product(exit_half, table_wide, False).astype(jnp.bfloat16)
    spectrum = left_product(table_tall, spread, False)
    modulus = jnp.sqrt(spectrum[:, 0] * spectrum[:, 0] + spectrum[:, 1] * spectrum[:, 1])
    scaling = amp_block.astype(jnp.float32) / jnp.maximum(modulus, 1.0)
    projected = (spectrum * scaling[:, None]).astype(jnp.bfloat16)
    back_half = right_product(projected, table_wide, True).astype(jnp.bfloat16)
    revised = left_product(table_tall, back_half, True)
    diff_real = revised[:, 0] - exit_real
    diff_imag = revised[:, 1] - exit_imag
    update_real = step_size * (probe_real * diff_real + probe_imag * diff_imag)
    update_imag = step_size * (probe_real * diff_imag - probe_imag * diff_real)
    patch_terms = jnp.stack([update_real, update_imag], axis=1)
    canvas = jnp.zeros(object_half.shape, jnp.float32)

    def place_one(counter, canvas_now):
        row_at = place_list[counter, 0]
        col_at = place_list[counter, 1]
        current = lax.dynamic_slice(canvas_now, (zero_index, row_at, col_at), (2, edge_width, edge_width))
        return lax.dynamic_update_slice(canvas_now, current + patch_terms[counter], (zero_index, row_at, col_at))
    return lax.fori_loop(0, place_list.shape[0], place_one, canvas)

def reference(objects, illumination, positions, amplitudes, projector):
    table_wide, table_tall = dft_tables(PSIZE)
    block_count = N_TILE * N_CUTS

    def per_angle(inputs):
        object_view, place_list, amp_list = inputs
        object_half = object_view.astype(jnp.bfloat16)

        def per_block(block_inputs):
            block_places, amp_block = block_inputs
            return patch_update(object_half, illumination, block_places, amp_block, table_wide, table_tall).astype(jnp.bfloat16)
        partials = lax.map(per_block, (place_list.reshape(block_count, PATCH_DEV, 2), amp_list.reshape(block_count, PATCH_DEV, PSIZE, PSIZE)))
        partials = lax.optimization_barrier(partials)
        summed = lax.optimization_barrier(jnp.sum(partials.astype(jnp.float32), axis=0))
        renewed = object_view + summed
        phase_image = (object_half[1].astype(jnp.float32) + summed[1]).astype(jnp.bfloat16)
        return (renewed, phase_image)
    new_objects, phase_images = lax.map(per_angle, (objects, positions, amplitudes))
    sinogram = jnp.transpose(phase_images, (1, 0, 2)).reshape(NPIX, ANGLES * NPIX)
    volume = jnp.dot(sinogram, projector, preferred_element_type=jnp.float32)
    return (new_objects, volume)
```

```python
import functools

import jax
import jax.numpy as jnp
import numpy as np
from jax import lax
from jax.experimental import pallas as pl
from jax.experimental.pallas import tpu as pltpu
from jax.sharding import PartitionSpec as P

step_size = 0.1
LANES = 128


def dft_blocks(width):
    index = np.arange(width)
    phase = (index[:, None] * index[None, :] % width) * (2.0 * np.pi / width)
    real = np.cos(phase) / np.sqrt(width)
    imag = -np.sin(phase) / np.sqrt(width)
    forward_right = np.block([[real, imag], [-imag, real]])
    forward_left = np.block([[real, -imag], [imag, real]])
    return (
        jnp.asarray(forward_right.astype(jnp.bfloat16)),
        jnp.asarray(forward_left.astype(jnp.bfloat16)),
    )


def dot(a, b):
    return jnp.dot(a, b, preferred_element_type=jnp.float32)


def patch_kernel(
    layout,
    place_ref,
    here_ref,
    *refs,
):
    (in_ids, out_ids, band_rows, tile_count, cuts_count) = layout
    n_in, n_out = len(in_ids), len(out_ids)
    piece_refs = refs[:n_in]
    probe_ref, amp_ref, right_ref, left_ref = refs[n_in : n_in + 4]
    out_refs = refs[n_in + 4 : n_in + 4 + n_out]
    image, canvas, exits = refs[n_in + 4 + n_out :]
    col_tiles = image.shape[1]
    edge = probe_ref.shape[-1]
    patches = amp_ref.shape[0]
    tile_at, cuts_at = here_ref[0], here_ref[1]

    def band_start(k, j):
        band = (tile_at ^ k) * cuts_count + (cuts_at ^ j)
        return pl.multiple_of(band * band_rows, band_rows)

    for ref, (plane, ks) in zip(piece_refs, in_ids):
        for slot, k in enumerate(ks):
            for j in range(cuts_count):
                rows = pl.ds(band_start(k, j), band_rows)
                for col in range(col_tiles):
                    image[plane, col, rows, :] = ref[
                        slot, j, :, col * LANES : (col + 1) * LANES
                    ].astype(jnp.float32)
    canvas[...] = jnp.zeros_like(canvas)
    lane = lax.broadcasted_iota(jnp.int32, (edge, LANES), 1)

    def pair(step, carry):
        spots = []
        for q in range(2):
            row_at = place_ref[2 * step + q, 0]
            col_at = place_ref[2 * step + q, 1]
            col = jnp.minimum(lax.div(col_at, LANES), col_tiles - 2)
            spots.append((row_at, col, col_at - col * LANES))
        probe_real, probe_imag = probe_ref[0], probe_ref[1]
        stacked = []
        for q, (row_at, col, shift) in enumerate(spots):
            back = (LANES - shift) & (LANES - 1)
            window = []
            for plane in range(2):
                near = image[plane, col, pl.ds(row_at, edge), :]
                far = image[plane, col + 1, pl.ds(row_at, edge), :]
                near = pltpu.roll(near, back, 1)
                far = pltpu.roll(far, back, 1)
                window.append(jnp.where(lane < LANES - shift, near, far))
            exit_real = probe_real * window[0] - probe_imag * window[1]
            exit_imag = probe_real * window[1] + probe_imag * window[0]
            exits[q, 0] = exit_real
            exits[q, 1] = exit_imag
            stacked.append(jnp.concatenate([exit_real, exit_imag], 1).astype(jnp.bfloat16))
        spread = dot(jnp.concatenate(stacked, 0), right_ref[...]).astype(jnp.bfloat16)

        def turn(x):
            top = jnp.concatenate([x[:edge, :edge], x[edge:, :edge]], 1)
            low = jnp.concatenate([x[:edge, edge:], x[edge:, edge:]], 1)
            return jnp.concatenate([top, low], 0)

        spectrum = dot(left_ref[...], turn(spread))
        real, imag = spectrum[:edge], spectrum[edge:]
        amp = jnp.concatenate([amp_ref[2 * step], amp_ref[2 * step + 1]], 1)
        scale = amp.astype(jnp.float32) * lax.rsqrt(jnp.maximum(real * real + imag * imag, 1.0))
        projected = jnp.concatenate([real * scale, imag * scale], 0).astype(jnp.bfloat16)
        back_half = dot(turn(projected), left_ref[...]).astype(jnp.bfloat16)
        revised = dot(right_ref[...], turn(back_half))
        for q, (row_at, col, shift) in enumerate(spots):
            diff_real = revised[:edge, q * edge : (q + 1) * edge] - exits[q, 0]
            diff_imag = revised[edge:, q * edge : (q + 1) * edge] - exits[q, 1]
            terms = (
                step_size * (probe_real * diff_real + probe_imag * diff_imag),
                step_size * (probe_real * diff_imag - probe_imag * diff_real),
            )
            for plane in range(2):
                moved = pltpu.roll(terms[plane], shift & (LANES - 1), 1)
                rows = pl.ds(row_at, edge)
                canvas[plane, col, rows, :] += jnp.where(lane >= shift, moved, 0.0)
                canvas[plane, col + 1, rows, :] += jnp.where(lane < shift, moved, 0.0)
        return carry

    lax.fori_loop(0, patches // 2, pair, 0)
    for ref, (plane, ks) in zip(out_refs, out_ids):
        for slot, k in enumerate(ks):
            for j in range(cuts_count):
                rows = pl.ds(band_start(k, j), band_rows)
                for col in range(col_tiles):
                    ref[slot, j, :, col * LANES : (col + 1) * LANES] = canvas[
                        plane, col, rows, :
                    ].astype(jnp.bfloat16)


def swap(x, axis, mask):
    size = lax.axis_size(axis)
    return lax.ppermute(x, axis, [(i, i ^ mask) for i in range(size)])


def add_up(*terms):
    total = terms[0].astype(jnp.float32)
    for term in terms[1:]:
        total = total + term.astype(jnp.float32)
    return total


def body(objects, illumination, positions, amplitudes, projector):
    cuts_count = lax.axis_size("cuts")
    tile_count = lax.axis_size("tile")
    angle_count = lax.axis_size("angle")
    band_rows, image_width = objects.shape[2:]
    edge = illumination.shape[-1]
    image_rows = band_rows * tile_count * cuts_count
    voxel_count = projector.shape[1]
    bits = [1 << i for i in range(tile_count.bit_length() - 1)]
    orders = (bits[::-1], bits)
    object_half = objects[0].astype(jnp.bfloat16)

    arrived = [swap(object_half, "cuts", j) for j in range(1, cuts_count)]
    held = [jnp.stack([object_half[plane]] + [a[plane] for a in arrived])[None] for plane in (0, 1)]
    held_ids = [(0,), (0,)]
    for stage in range(len(bits)):
        got = [swap(held[plane], "tile", orders[plane][stage]) for plane in (0, 1)]
        if stage == len(bits) - 1:
            pieces = []
            for plane in (0, 1):
                bit = orders[plane][stage]
                pieces.append((held[plane], plane, held_ids[plane]))
                pieces.append((got[plane], plane, tuple(k ^ bit for k in held_ids[plane])))
        else:
            for plane in (0, 1):
                bit = orders[plane][stage]
                held[plane] = jnp.concatenate([held[plane], got[plane]])
                held_ids[plane] = held_ids[plane] + tuple(k ^ bit for k in held_ids[plane])

    out_ids = []
    for plane in (0, 1):
        bit = orders[plane][0]
        out_ids.append((plane, tuple(k for k in range(tile_count) if not k & bit)))
        out_ids.append((plane, tuple(k for k in range(tile_count) if k & bit)))
    layout = (
        tuple((plane, ids) for _, plane, ids in pieces),
        tuple(out_ids),
        band_rows,
        tile_count,
        cuts_count,
    )
    right_block, left_block = dft_blocks(edge)
    here = jnp.stack([lax.axis_index("tile"), lax.axis_index("cuts")]).astype(jnp.int32)
    vmem = pl.BlockSpec(memory_space=pltpu.VMEM)
    smem = pl.BlockSpec(memory_space=pltpu.SMEM)
    col_tiles = image_width // LANES
    outs = pl.pallas_call(
        functools.partial(patch_kernel, layout),
        out_shape=[
            jax.ShapeDtypeStruct((len(ks), cuts_count, band_rows, image_width), jnp.bfloat16)
            for _, ks in out_ids
        ],
        in_specs=[smem, smem] + [vmem] * (len(pieces) + 4),
        out_specs=[vmem] * len(out_ids),
        scratch_shapes=[
            pltpu.VMEM((2, col_tiles, image_rows, LANES), jnp.float32),
            pltpu.VMEM((2, col_tiles, image_rows, LANES), jnp.float32),
            pltpu.VMEM((2, 2, edge, edge), jnp.float32),
        ],
    )(
        positions[0],
        here,
        *[piece for piece, _, _ in pieces],
        illumination,
        amplitudes[0],
        right_block,
        left_block,
    )

    keep = [outs[0], outs[2]]
    send = [outs[1], outs[3]]
    keep_ids = [out_ids[0][1], out_ids[2][1]]
    for stage in range(len(bits)):
        got = [None, None]
        for plane in (1, 0):
            got[plane] = swap(send[plane], "tile", orders[plane][stage])
        for plane in (1, 0):
            total = add_up(keep[plane], got[plane]).astype(jnp.bfloat16)
            if stage == len(bits) - 1:
                keep[plane] = total[0]
                continue
            bit = orders[plane][stage + 1]
            stay = [i for i, k in enumerate(keep_ids[plane]) if not k & bit]
            leave = [i for i, k in enumerate(keep_ids[plane]) if k & bit]
            keep_ids[plane] = tuple(keep_ids[plane][i] for i in stay)
            keep[plane] = jnp.stack([total[i] for i in stay])
            send[plane] = jnp.stack([total[i] for i in leave])
    share = [None, None]
    for plane in (1, 0):
        got = [swap(keep[plane][j], "cuts", j) for j in range(1, cuts_count)]
        share[plane] = add_up(keep[plane][0], *got)
    new_objects = objects + jnp.stack(share)[None]
    phase = (object_half[1].astype(jnp.float32) + share[1]).astype(jnp.bfloat16)

    rows = jnp.stack([phase] + [swap(phase, "cuts", j) for j in range(1, cuts_count)])
    cuts_at = lax.axis_index("cuts")
    angle_at = lax.axis_index("angle")
    by_angle = [rows] + [swap(rows, "angle", a) for a in range(1, angle_count)]
    weights = projector.reshape(angle_count, image_width, voxel_count)
    total = None
    for a in range(angle_count):
        weight = lax.dynamic_index_in_dim(weights, angle_at ^ a, 0, keepdims=False)
        part = dot(by_angle[a].reshape(cuts_count * band_rows, image_width), weight)
        total = part if total is None else total + part
    total = total.reshape(cuts_count, band_rows, voxel_count)
    volume = jnp.take(total, jnp.arange(cuts_count) ^ cuts_at, axis=0)
    return new_objects, volume.reshape(cuts_count * band_rows, voxel_count)


def solution(mesh):
    in_specs = (
        P("angle", None, ("tile", "cuts"), None),
        P(),
        P("angle", ("tile", "cuts"), None),
        P("angle", ("tile", "cuts"), None, None),
        P(None, ("angle", "cuts")),
    )
    out_specs = (P("angle", None, ("tile", "cuts"), None), P("tile", ("angle", "cuts")))
    return jax.shard_map(body, mesh=mesh, in_specs=in_specs, out_specs=out_specs, check_vma=False)
```

```python
import functools

import jax
import jax.numpy as jnp
import numpy as np
from jax import lax
from jax.experimental import pallas as pl
from jax.experimental.pallas import tpu as pltpu
from jax.sharding import PartitionSpec as P

step_size = 0.1
LANES = 128
GROUP = 16
VMEM_LIMIT = 24 * 2**20


def dft_blocks(width):
    index = np.arange(width)
    phase = (index[:, None] * index[None, :] % width) * (2.0 * np.pi / width)
    real = np.cos(phase) / np.sqrt(width)
    imag = -np.sin(phase) / np.sqrt(width)
    forward_right = np.block([[real, imag], [-imag, real]])
    forward_left = np.block([[real, -imag], [imag, real]])
    return (
        jnp.asarray(forward_right.astype(jnp.bfloat16)),
        jnp.asarray(forward_left.astype(jnp.bfloat16)),
    )


def dot(a, b):
    return jnp.dot(a, b, preferred_element_type=jnp.float32)


def patch_kernel(
    layout,
    place_ref,
    here_ref,
    *refs,
):
    (in_ids, out_ids, band_rows, tile_count, cuts_count, group) = layout
    n_in, n_out = len(in_ids), len(out_ids)
    piece_refs = refs[:n_in]
    probe_ref, amp_ref, right_ref, left_ref = refs[n_in : n_in + 4]
    out_refs = refs[n_in + 4 : n_in + 4 + n_out]
    image, canvas, exits = refs[n_in + 4 + n_out :]
    col_tiles = image.shape[1]
    edge = probe_ref.shape[-1]
    patches = amp_ref.shape[0]
    tile_at, cuts_at = here_ref[0], here_ref[1]

    def band_start(k, j):
        band = (tile_at ^ k) * cuts_count + (cuts_at ^ j)
        return pl.multiple_of(band * band_rows, band_rows)

    for ref, spots in zip(piece_refs, in_ids):
        for slot, (k, j) in enumerate(spots):
            rows = pl.ds(band_start(k, j), band_rows)
            for plane in range(2):
                for col in range(col_tiles):
                    image[plane, col, rows, :] = ref[
                        slot, plane, :, col * LANES : (col + 1) * LANES
                    ].astype(jnp.float32)
    canvas[...] = jnp.zeros_like(canvas)
    lane = lax.broadcasted_iota(jnp.int32, (edge, LANES), 1)

    def several(step, carry):
        spots = []
        for q in range(group):
            row_at = place_ref[group * step + q, 0]
            col_at = place_ref[group * step + q, 1]
            col = jnp.minimum(lax.div(col_at, LANES), col_tiles - 2)
            spots.append((pl.ds(row_at, edge), col, col_at - col * LANES))
        probe_real, probe_imag = probe_ref[0], probe_ref[1]
        stacked = []
        for q, (rows, col, shift) in enumerate(spots):
            back = (LANES - shift) & (LANES - 1)
            window = []
            for plane in range(2):
                near = image[plane, col, rows, :]
                far = image[plane, col + 1, rows, :]
                window.append(pltpu.roll(jnp.where(lane < shift, far, near), back, 1))
            exit_real = probe_real * window[0] - probe_imag * window[1]
            exit_imag = probe_real * window[1] + probe_imag * window[0]
            exits[q, 0] = exit_real
            exits[q, 1] = exit_imag
            stacked.append(jnp.concatenate([exit_real, exit_imag], 1).astype(jnp.bfloat16))
        spread = dot(jnp.concatenate(stacked, 0), right_ref[...]).astype(jnp.bfloat16)

        def side_by_side(x):
            halves = [
                jnp.concatenate(
                    [x[q * edge : (q + 1) * edge, h * edge : (h + 1) * edge] for q in range(group)], 1
                )
                for h in range(2)
            ]
            return jnp.concatenate(halves, 0)

        spectrum = dot(left_ref[...], side_by_side(spread))
        real, imag = spectrum[:edge], spectrum[edge:]
        amp = jnp.concatenate([amp_ref[group * step + q] for q in range(group)], 1)
        scale = amp.astype(jnp.float32) * lax.rsqrt(jnp.maximum(real * real + imag * imag, 1.0))
        real = (real * scale).astype(jnp.bfloat16)
        imag = (imag * scale).astype(jnp.bfloat16)
        projected = jnp.concatenate(
            [
                jnp.concatenate([part[:, q * edge : (q + 1) * edge] for part in (real, imag)], 1)
                for q in range(group)
            ],
            0,
        )
        back_half = dot(projected, left_ref[...]).astype(jnp.bfloat16)
        revised = dot(right_ref[...], side_by_side(back_half))
        for q, (rows, col, shift) in enumerate(spots):
            diff_real = revised[:edge, q * edge : (q + 1) * edge] - exits[q, 0]
            diff_imag = revised[edge:, q * edge : (q + 1) * edge] - exits[q, 1]
            terms = (
                step_size * (probe_real * diff_real + probe_imag * diff_imag),
                step_size * (probe_real * diff_imag - probe_imag * diff_real),
            )
            for plane in range(2):
                moved = pltpu.roll(terms[plane], shift & (LANES - 1), 1)
                near = canvas[plane, col, rows, :] + jnp.where(lane >= shift, moved, 0.0)
                far = canvas[plane, col + 1, rows, :] + jnp.where(lane < shift, moved, 0.0)
                canvas[plane, col, rows, :] = near
                canvas[plane, col + 1, rows, :] = far
        return carry

    lax.fori_loop(0, patches // group, several, 0)
    for ref, (plane, k) in zip(out_refs, out_ids):
        for j in range(cuts_count):
            rows = pl.ds(band_start(k, j), band_rows)
            for col in range(col_tiles):
                ref[j, :, col * LANES : (col + 1) * LANES] = canvas[plane, col, rows, :].astype(
                    jnp.bfloat16
                )


def volume_kernel(angle_count, cuts_count, at_ref, *refs):
    phase_refs = refs[:angle_count]
    weight_ref, out_ref, rows_ref = refs[angle_count:]
    cuts_at, angle_at = at_ref[0], at_ref[1]
    band_rows, width = phase_refs[0].shape[1:]
    total = None
    for a, ref in enumerate(phase_refs):
        for j in range(cuts_count):
            rows = pl.ds(pl.multiple_of((cuts_at ^ j) * band_rows, band_rows), band_rows)
            rows_ref[a, rows, :] = ref[j]
        weight = weight_ref[pl.ds(pl.multiple_of((angle_at ^ a) * width, width), width), :]
        part = dot(rows_ref[a], weight)
        total = part if total is None else total + part
    out_ref[...] = total


def swap(x, axis, mask):
    size = lax.axis_size(axis)
    return lax.ppermute(x, axis, [(i, i ^ mask) for i in range(size)])


def add_up(*terms):
    total = terms[0].astype(jnp.float32)
    for term in terms[1:]:
        total = total + term.astype(jnp.float32)
    return total


def body(objects, illumination, positions, amplitudes, projector):
    cuts_count = lax.axis_size("cuts")
    tile_count = lax.axis_size("tile")
    angle_count = lax.axis_size("angle")
    band_rows, image_width = objects.shape[2:]
    edge = illumination.shape[-1]
    image_rows = band_rows * tile_count * cuts_count
    voxel_count = projector.shape[1]
    object_half = objects[0].astype(jnp.bfloat16)

    near = [object_half] + [swap(object_half, "cuts", j) for j in range(1, cuts_count)]
    far = jnp.stack(near[1:])
    pieces = [(object_half[None], ((0, 0),)), (far, tuple((0, j) for j in range(1, cuts_count)))]
    for k in range(1, tile_count):
        pieces.append((swap(object_half, "tile", k)[None], ((k, 0),)))
    for k in range(1, tile_count):
        pieces.append((swap(far, "tile", k), tuple((k, j) for j in range(1, cuts_count))))

    out_ids = tuple((plane, k) for plane in (1, 0) for k in range(tile_count))
    group = next(g for g in (GROUP, 8, 4, 2, 1) if amplitudes.shape[1] % g == 0)
    layout = (tuple(ids for _, ids in pieces), out_ids, band_rows, tile_count, cuts_count, group)
    right_block, left_block = dft_blocks(edge)
    tile_at, cuts_at, angle_at = (lax.axis_index(axis) for axis in ("tile", "cuts", "angle"))
    here = jnp.stack([tile_at, cuts_at]).astype(jnp.int32)
    vmem = pl.BlockSpec(memory_space=pltpu.VMEM)
    smem = pl.BlockSpec(memory_space=pltpu.SMEM)
    col_tiles = image_width // LANES
    outs = pl.pallas_call(
        functools.partial(patch_kernel, layout),
        out_shape=[
            jax.ShapeDtypeStruct((cuts_count, band_rows, image_width), jnp.bfloat16)
            for _ in out_ids
        ],
        in_specs=[smem, smem] + [vmem] * (len(pieces) + 4),
        out_specs=[vmem] * len(out_ids),
        scratch_shapes=[
            pltpu.VMEM((2, col_tiles, image_rows, LANES), jnp.float32),
            pltpu.VMEM((2, col_tiles, image_rows, LANES), jnp.float32),
            pltpu.VMEM((group, 2, edge, edge), jnp.float32),
        ],
        compiler_params=pltpu.CompilerParams(vmem_limit_bytes=VMEM_LIMIT),
    )(
        positions[0],
        here,
        *[piece for piece, _ in pieces],
        illumination,
        amplitudes[0],
        right_block,
        left_block,
    )
    imag_outs, real_outs = outs[:tile_count], outs[tile_count:]

    imag_part, real_part = (
        add_up(part[0], *[swap(part[k], "tile", k) for k in range(1, tile_count)]).astype(jnp.bfloat16)
        for part in (imag_outs, real_outs)
    )
    imag_sum = add_up(imag_part[0], *[swap(imag_part[j], "cuts", j) for j in range(1, cuts_count)])[None]
    own_real = add_up(real_part[0], *[swap(real_part[j], "cuts", j) for j in range(1, cuts_count)])
    share = jnp.stack([own_real, imag_sum[0]])
    new_objects = objects + share[None]
    phase = (object_half[1].astype(jnp.float32) + imag_sum).astype(jnp.bfloat16)
    own_phase = phase[0]
    phase = jnp.stack([own_phase] + [swap(own_phase, "cuts", j) for j in range(1, cuts_count)])
    by_angle = [phase] + [swap(phase, "angle", a) for a in range(1, angle_count)]
    volume = pl.pallas_call(
        functools.partial(volume_kernel, angle_count, cuts_count),
        out_shape=jax.ShapeDtypeStruct((cuts_count * band_rows, voxel_count), jnp.float32),
        in_specs=[smem] + [vmem] * (angle_count + 1),
        out_specs=vmem,
        scratch_shapes=[pltpu.VMEM((angle_count, cuts_count * band_rows, image_width), jnp.bfloat16)],
        compiler_params=pltpu.CompilerParams(vmem_limit_bytes=VMEM_LIMIT),
    )(jnp.stack([cuts_at, angle_at]).astype(jnp.int32), *by_angle, projector)
    return new_objects, volume


def solution(mesh):
    in_specs = (
        P("angle", None, ("tile", "cuts"), None),
        P(),
        P("angle", ("tile", "cuts"), None),
        P("angle", ("tile", "cuts"), None, None),
        P(None, ("angle", "cuts")),
    )
    out_specs = (P("angle", None, ("tile", "cuts"), None), P("tile", ("angle", "cuts")))
    return jax.shard_map(body, mesh=mesh, in_specs=in_specs, out_specs=out_specs, check_vma=False)
```

```python
import functools

import jax
import jax.numpy as jnp
import numpy as np
from jax import lax
from jax.experimental import pallas as pl
from jax.experimental.pallas import tpu as pltpu
from jax.sharding import PartitionSpec as P


step_size = 0.1
LANES = 128
GROUP = 16
VMEM_LIMIT = 24 * 2**20


def dft_table(width):
    index = np.arange(width)
    phase = (index[:, None] * index[None, :] % width) * (2.0 * np.pi / width)
    real = np.cos(phase) / np.sqrt(width)
    imag = -np.sin(phase) / np.sqrt(width)
    return jnp.asarray(np.stack([real, imag]).astype(jnp.bfloat16))


def dot(a, b):
    return jnp.dot(a, b, preferred_element_type=jnp.float32)


def patch_kernel(
    layout,
    place_ref,
    here_ref,
    *refs,
):
    (in_ids, out_ids, band_rows, _, cuts_count, group) = layout
    n_in, n_out = len(in_ids), len(out_ids)
    piece_refs = refs[:n_in]
    probe_ref, amp_ref, table_ref = refs[n_in : n_in + 3]
    out_refs = refs[n_in + 3 : n_in + 3 + n_out]
    image, canvas, exits, right_ref, left_ref = refs[n_in + 3 + n_out :]
    col_tiles = image.shape[1]
    edge = probe_ref.shape[-1]
    patches = amp_ref.shape[0]
    tile_at, cuts_at = here_ref[0], here_ref[1]

    def band_start(k, j):
        band = (tile_at ^ k) * cuts_count + (cuts_at ^ j)
        return pl.multiple_of(band * band_rows, band_rows)

    for ref, spots in zip(piece_refs, in_ids):
        for slot, (k, j) in enumerate(spots):
            rows = pl.ds(band_start(k, j), band_rows)
            for plane in range(2):
                for col in range(col_tiles):
                    image[plane, col, rows, :] = ref[
                        slot, plane, :, col * LANES : (col + 1) * LANES
                    ].astype(jnp.float32)
    canvas[...] = jnp.zeros_like(canvas)
    for top in range(2):
        for side in range(2):
            block = table_ref[top ^ side]
            here = (slice(top * edge, (top + 1) * edge), slice(side * edge, (side + 1) * edge))
            right_ref[here] = -block if top > side else block
            left_ref[here] = -block if top < side else block
    lane = lax.broadcasted_iota(jnp.int32, (edge, LANES), 1)

    def several(step, carry):
        spots = []
        for q in range(group):
            row_at = place_ref[group * step + q, 0]
            col_at = place_ref[group * step + q, 1]
            col = jnp.minimum(lax.div(col_at, LANES), col_tiles - 2)
            spots.append((pl.ds(row_at, edge), col, col_at - col * LANES))
        probe_real, probe_imag = probe_ref[0], probe_ref[1]
        stacked = []
        for q, (rows, col, shift) in enumerate(spots):
            back = (LANES - shift) & (LANES - 1)
            window = []
            for plane in range(2):
                near = image[plane, col, rows, :]
                far = image[plane, col + 1, rows, :]
                window.append(pltpu.roll(jnp.where(lane < shift, far, near), back, 1))
            exit_real = probe_real * window[0] - probe_imag * window[1]
            exit_imag = probe_real * window[1] + probe_imag * window[0]
            exits[q, 0] = exit_real
            exits[q, 1] = exit_imag
            stacked.append(jnp.concatenate([exit_real, exit_imag], 1).astype(jnp.bfloat16))
        spread = dot(jnp.concatenate(stacked, 0), right_ref[...]).astype(jnp.bfloat16)

        def side_by_side(x):
            halves = [
                jnp.concatenate(
                    [x[q * edge : (q + 1) * edge, h * edge : (h + 1) * edge] for q in range(group)], 1
                )
                for h in range(2)
            ]
            return jnp.concatenate(halves, 0)

        spectrum = dot(left_ref[...], side_by_side(spread))
        real, imag = spectrum[:edge], spectrum[edge:]
        amp = jnp.concatenate([amp_ref[group * step + q] for q in range(group)], 1)
        scale = amp.astype(jnp.float32) * lax.rsqrt(jnp.maximum(real * real + imag * imag, 1.0))
        real = (real * scale).astype(jnp.bfloat16)
        imag = (imag * scale).astype(jnp.bfloat16)
        projected = jnp.concatenate(
            [
                jnp.concatenate([part[:, q * edge : (q + 1) * edge] for part in (real, imag)], 1)
                for q in range(group)
            ],
            0,
        )
        back_half = dot(projected, left_ref[...]).astype(jnp.bfloat16)
        revised = dot(right_ref[...], side_by_side(back_half))
        for q, (rows, col, shift) in enumerate(spots):
            diff_real = revised[:edge, q * edge : (q + 1) * edge] - exits[q, 0]
            diff_imag = revised[edge:, q * edge : (q + 1) * edge] - exits[q, 1]
            terms = (
                step_size * (probe_real * diff_real + probe_imag * diff_imag),
                step_size * (probe_real * diff_imag - probe_imag * diff_real),
            )
            for plane in range(2):
                moved = pltpu.roll(terms[plane], shift & (LANES - 1), 1)
                near = canvas[plane, col, rows, :] + jnp.where(lane >= shift, moved, 0.0)
                far = canvas[plane, col + 1, rows, :] + jnp.where(lane < shift, moved, 0.0)
                canvas[plane, col, rows, :] = near
                canvas[plane, col + 1, rows, :] = far
        return carry

    lax.fori_loop(0, patches // group, several, 0)
    for ref, (plane, k) in zip(out_refs, out_ids):
        for j in range(cuts_count):
            rows = pl.ds(band_start(k, j), band_rows)
            for col in range(col_tiles):
                ref[j, :, col * LANES : (col + 1) * LANES] = canvas[plane, col, rows, :].astype(
                    jnp.bfloat16
                )


def volume_kernel(masks, cuts_count, at_ref, *refs):
    phase_refs = refs[: len(masks)]
    weight_ref, out_ref, rows_ref = refs[-3:]
    cuts_at, angle_at = at_ref[0], at_ref[1]
    band_rows, width = phase_refs[0].shape[1:]
    total = refs[len(masks)][...] if len(refs) > len(masks) + 3 else None
    for a, (mask, ref) in enumerate(zip(masks, phase_refs)):
        for j in range(cuts_count):
            rows = pl.ds(pl.multiple_of((cuts_at ^ j) * band_rows, band_rows), band_rows)
            rows_ref[a, rows, :] = ref[j]
        weight = weight_ref[pl.ds(pl.multiple_of((angle_at ^ mask) * width, width), width), :]
        part = dot(rows_ref[a], weight)
        total = part if total is None else total + part
    out_ref[...] = total


def swap(x, axis, mask):
    size = lax.axis_size(axis)
    return lax.ppermute(x, axis, [(i, i ^ mask) for i in range(size)])


def add_up(*terms):
    total = terms[0].astype(jnp.float32)
    for term in terms[1:]:
        total = total + term.astype(jnp.float32)
    return total


def compute(objects, illumination, positions, amplitudes, projector):
    cuts_count = lax.axis_size("cuts")
    tile_count = lax.axis_size("tile")
    angle_count = lax.axis_size("angle")
    band_rows, image_width = objects.shape[2:]
    edge = illumination.shape[-1]
    image_rows = band_rows * tile_count * cuts_count
    voxel_count = projector.shape[1]
    object_half = objects[0].astype(jnp.bfloat16)

    near = [object_half]
    for j in range(1, cuts_count):
        near.append(swap(object_half, "cuts", j))
    own_spread = []
    for k in range(1, tile_count):
        own_spread.append(swap(object_half, "tile", k))
    far = jnp.stack(near[1:])
    pieces = [(object_half[None], ((0, 0),)), (far, tuple((0, j) for j in range(1, cuts_count)))]
    pieces += [(own_spread[k - 1][None], ((k, 0),)) for k in range(1, tile_count)]
    for k in range(1, tile_count):
        pieces.append((swap(far, "tile", k), tuple((k, j) for j in range(1, cuts_count))))

    out_ids = tuple((plane, k) for plane in (1, 0) for k in range(tile_count))
    group = next(g for g in (GROUP, 8, 4, 2, 1) if amplitudes.shape[1] % g == 0)
    layout = (tuple(ids for _, ids in pieces), out_ids, band_rows, tile_count, cuts_count, group)
    tile_at, cuts_at, angle_at = (lax.axis_index(axis) for axis in ("tile", "cuts", "angle"))
    here = jnp.stack([tile_at, cuts_at]).astype(jnp.int32)
    vmem = pl.BlockSpec(memory_space=pltpu.VMEM)
    smem = pl.BlockSpec(memory_space=pltpu.SMEM)
    col_tiles = image_width // LANES
    outs = pl.pallas_call(
        functools.partial(patch_kernel, layout),
        out_shape=[
            jax.ShapeDtypeStruct((cuts_count, band_rows, image_width), jnp.bfloat16)
            for _ in out_ids
        ],
        in_specs=[smem, smem] + [vmem] * (len(pieces) + 3),
        out_specs=[vmem] * len(out_ids),
        scratch_shapes=[
            pltpu.VMEM((2, col_tiles, image_rows, LANES), jnp.float32),
            pltpu.VMEM((2, col_tiles, image_rows, LANES), jnp.float32),
            pltpu.VMEM((group, 2, edge, edge), jnp.float32),
            pltpu.VMEM((2 * edge, 2 * edge), jnp.bfloat16),
            pltpu.VMEM((2 * edge, 2 * edge), jnp.bfloat16),
        ],
        compiler_params=pltpu.CompilerParams(vmem_limit_bytes=VMEM_LIMIT),
    )(
        positions[0],
        here,
        *[piece for piece, _ in pieces],
        illumination,
        amplitudes[0],
        dft_table(edge),
    )
    imag_outs, real_outs = outs[:tile_count], outs[tile_count:]

    imag_part, real_part = (
        add_up(part[0], *[swap(part[k], "tile", k) for k in range(1, tile_count)]).astype(jnp.bfloat16)
        for part in (imag_outs, real_outs)
    )
    imag_sum = add_up(imag_part[0], *[swap(imag_part[j], "cuts", j) for j in range(1, cuts_count)])[None]
    own_real = add_up(real_part[0], *[swap(real_part[j], "cuts", j) for j in range(1, cuts_count)])
    share = jnp.stack([own_real, imag_sum[0]])
    new_objects = objects + share[None]
    phase = (object_half[1].astype(jnp.float32) + imag_sum).astype(jnp.bfloat16)
    own_phase = phase[0]
    rows = [own_phase]
    for j in range(1, cuts_count):
        rows.append(swap(own_phase, "cuts", j))
    phase = jnp.stack(rows)
    others = [swap(phase, "angle", a) for a in range(1, angle_count)]
    at = jnp.stack([cuts_at, angle_at]).astype(jnp.int32)
    volume_rows = cuts_count * band_rows

    def product(masks, blocks, *before):
        return pl.pallas_call(
            functools.partial(volume_kernel, masks, cuts_count),
            out_shape=jax.ShapeDtypeStruct((volume_rows, voxel_count), jnp.float32),
            in_specs=[smem] + [vmem] * (len(blocks) + len(before) + 1),
            out_specs=vmem,
            scratch_shapes=[pltpu.VMEM((len(masks), volume_rows, image_width), jnp.bfloat16)],
            compiler_params=pltpu.CompilerParams(vmem_limit_bytes=VMEM_LIMIT),
        )(at, *blocks, *before, projector)

    volume = product((0,), (phase,))
    if angle_count > 1:
        volume = product(tuple(range(1, angle_count)), others, volume)
    return new_objects, volume


def solution(mesh):
    in_specs = (
        P("angle", None, ("tile", "cuts"), None),
        P(),
        P("angle", ("tile", "cuts"), None),
        P("angle", ("tile", "cuts"), None, None),
        P(None, ("angle", "cuts")),
    )
    out_specs = (P("angle", None, ("tile", "cuts"), None), P("tile", ("angle", "cuts")))
    return jax.shard_map(compute, mesh=mesh, in_specs=in_specs, out_specs=out_specs, check_vma=False)
```

```python
import functools

import jax
import jax.numpy as jnp
import numpy as np
from jax import lax
from jax.experimental import pallas as pl
from jax.experimental.pallas import tpu as pltpu
from jax.sharding import PartitionSpec as P


step_size = 0.1
LANES = 128
GROUP = 16
VMEM_LIMIT = 24 * 2**20


def dft_table(width):
    index = np.arange(width)
    phase = (index[:, None] * index[None, :] % width) * (2.0 * np.pi / width)
    real = np.cos(phase) / np.sqrt(width)
    imag = -np.sin(phase) / np.sqrt(width)
    return jnp.asarray(np.stack([real, imag]).astype(jnp.bfloat16))


def dot(a, b):
    return jnp.dot(a, b, preferred_element_type=jnp.float32)


def patch_kernel(
    layout,
    place_ref,
    *refs,
):
    (in_ids, out_ids, band_rows, _, cuts_count, group) = layout
    n_in, n_out = len(in_ids), len(out_ids)
    piece_refs = refs[:n_in]
    probe_ref, amp_ref, table_ref = refs[n_in : n_in + 3]
    out_refs = refs[n_in + 3 : n_in + 3 + n_out]
    image, canvas, exits, right_ref, left_ref, places, place_sem = refs[n_in + 3 + n_out :]
    fetch = pltpu.make_async_copy(place_ref, places, place_sem)
    fetch.start()
    col_tiles = image.shape[1]
    edge = probe_ref.shape[-1]
    patches = amp_ref.shape[0]
    tile_at, cuts_at = lax.axis_index("tile"), lax.axis_index("cuts")

    def band_start(k, j):
        band = (tile_at ^ k) * cuts_count + (cuts_at ^ j)
        return pl.multiple_of(band * band_rows, band_rows)

    for ref, spots in zip(piece_refs, in_ids):
        for slot, (k, j) in enumerate(spots):
            rows = pl.ds(band_start(k, j), band_rows)
            for plane in range(2):
                for col in range(col_tiles):
                    image[plane, col, rows, :] = ref[
                        slot, plane, :, col * LANES : (col + 1) * LANES
                    ].astype(jnp.float32)
    canvas[...] = jnp.zeros_like(canvas)
    for top in range(2):
        for side in range(2):
            block = table_ref[top ^ side]
            here = (slice(top * edge, (top + 1) * edge), slice(side * edge, (side + 1) * edge))
            right_ref[here] = -block if top > side else block
            left_ref[here] = -block if top < side else block
    lane = lax.broadcasted_iota(jnp.int32, (edge, LANES), 1)

    def several(step, carry):
        spots = []
        for q in range(group):
            row_at = places[group * step + q, 0]
            col_at = places[group * step + q, 1]
            col = jnp.minimum(lax.div(col_at, LANES), col_tiles - 2)
            spots.append((pl.ds(row_at, edge), col, col_at - col * LANES))
        probe_real, probe_imag = probe_ref[0], probe_ref[1]
        stacked = []
        for q, (rows, col, shift) in enumerate(spots):
            back = (LANES - shift) & (LANES - 1)
            window = []
            for plane in range(2):
                near = image[plane, col, rows, :]
                far = image[plane, col + 1, rows, :]
                window.append(pltpu.roll(jnp.where(lane < shift, far, near), back, 1))
            exit_real = probe_real * window[0] - probe_imag * window[1]
            exit_imag = probe_real * window[1] + probe_imag * window[0]
            exits[q, 0] = exit_real
            exits[q, 1] = exit_imag
            stacked.append(jnp.concatenate([exit_real, exit_imag], 1).astype(jnp.bfloat16))
        spread = dot(jnp.concatenate(stacked, 0), right_ref[...]).astype(jnp.bfloat16)

        def side_by_side(x):
            halves = [
                jnp.concatenate(
                    [x[q * edge : (q + 1) * edge, h * edge : (h + 1) * edge] for q in range(group)], 1
                )
                for h in range(2)
            ]
            return jnp.concatenate(halves, 0)

        spectrum = dot(left_ref[...], side_by_side(spread))
        real, imag = spectrum[:edge], spectrum[edge:]
        amp = jnp.concatenate([amp_ref[group * step + q] for q in range(group)], 1)
        scale = amp.astype(jnp.float32) * lax.rsqrt(jnp.maximum(real * real + imag * imag, 1.0))
        real = (real * scale).astype(jnp.bfloat16)
        imag = (imag * scale).astype(jnp.bfloat16)
        projected = jnp.concatenate(
            [
                jnp.concatenate([part[:, q * edge : (q + 1) * edge] for part in (real, imag)], 1)
                for q in range(group)
            ],
            0,
        )
        back_half = dot(projected, left_ref[...]).astype(jnp.bfloat16)
        revised = dot(right_ref[...], side_by_side(back_half))
        for q, (rows, col, shift) in enumerate(spots):
            diff_real = revised[:edge, q * edge : (q + 1) * edge] - exits[q, 0]
            diff_imag = revised[edge:, q * edge : (q + 1) * edge] - exits[q, 1]
            terms = (
                step_size * (probe_real * diff_real + probe_imag * diff_imag),
                step_size * (probe_real * diff_imag - probe_imag * diff_real),
            )
            for plane in range(2):
                moved = pltpu.roll(terms[plane], shift & (LANES - 1), 1)
                near = canvas[plane, col, rows, :] + jnp.where(lane >= shift, moved, 0.0)
                far = canvas[plane, col + 1, rows, :] + jnp.where(lane < shift, moved, 0.0)
                canvas[plane, col, rows, :] = near
                canvas[plane, col + 1, rows, :] = far
        return carry

    fetch.wait()
    lax.fori_loop(0, patches // group, several, 0)
    for ref, (plane, k) in zip(out_refs, out_ids):
        for j in range(cuts_count):
            rows = pl.ds(band_start(k, j), band_rows)
            for col in range(col_tiles):
                ref[j, :, col * LANES : (col + 1) * LANES] = canvas[plane, col, rows, :].astype(
                    jnp.bfloat16
                )


def volume_kernel(masks, cuts_count, *refs):
    phase_refs = refs[: len(masks)]
    weight_ref, out_ref, rows_ref = refs[-3:]
    cuts_at, angle_at = lax.axis_index("cuts"), lax.axis_index("angle")
    band_rows, width = phase_refs[0].shape[1:]
    total = refs[len(masks)][...] if len(refs) > len(masks) + 3 else None
    for a, (mask, ref) in enumerate(zip(masks, phase_refs)):
        for j in range(cuts_count):
            rows = pl.ds(pl.multiple_of((cuts_at ^ j) * band_rows, band_rows), band_rows)
            rows_ref[a, rows, :] = ref[j]
        weight = weight_ref[pl.ds(pl.multiple_of((angle_at ^ mask) * width, width), width), :]
        part = dot(rows_ref[a], weight)
        total = part if total is None else total + part
    out_ref[...] = total


def swap(x, axis, mask):
    size = lax.axis_size(axis)
    return lax.ppermute(x, axis, [(i, i ^ mask) for i in range(size)])


def add_up(*terms):
    total = terms[0].astype(jnp.float32)
    for term in terms[1:]:
        total = total + term.astype(jnp.float32)
    return total


def compute(objects, illumination, positions, amplitudes, projector):
    cuts_count = lax.axis_size("cuts")
    tile_count = lax.axis_size("tile")
    angle_count = lax.axis_size("angle")
    band_rows, image_width = objects.shape[2:]
    edge = illumination.shape[-1]
    image_rows = band_rows * tile_count * cuts_count
    voxel_count = projector.shape[1]
    object_half = objects[0].astype(jnp.bfloat16)

    near = [object_half]
    for j in range(1, cuts_count):
        near.append(swap(object_half, "cuts", j))
    own_spread = []
    for k in range(1, tile_count):
        own_spread.append(swap(object_half, "tile", k))
    far = jnp.stack(near[1:])
    pieces = [(object_half[None], ((0, 0),)), (far, tuple((0, j) for j in range(1, cuts_count)))]
    pieces += [(own_spread[k - 1][None], ((k, 0),)) for k in range(1, tile_count)]
    for k in range(1, tile_count):
        pieces.append((swap(far, "tile", k), tuple((k, j) for j in range(1, cuts_count))))

    out_ids = tuple((plane, k) for plane in (1, 0) for k in range(tile_count))
    group = next(g for g in (GROUP, 8, 4, 2, 1) if amplitudes.shape[1] % g == 0)
    layout = (tuple(ids for _, ids in pieces), out_ids, band_rows, tile_count, cuts_count, group)
    vmem = pl.BlockSpec(memory_space=pltpu.VMEM)
    smem = pl.BlockSpec(memory_space=pltpu.SMEM)
    col_tiles = image_width // LANES
    outs = pl.pallas_call(
        functools.partial(patch_kernel, layout),
        out_shape=[
            jax.ShapeDtypeStruct((cuts_count, band_rows, image_width), jnp.bfloat16)
            for _ in out_ids
        ],
        in_specs=[pl.BlockSpec(memory_space=pl.ANY)] + [vmem] * (len(pieces) + 3),
        out_specs=[vmem] * len(out_ids),
        scratch_shapes=[
            pltpu.VMEM((2, col_tiles, image_rows, LANES), jnp.float32),
            pltpu.VMEM((2, col_tiles, image_rows, LANES), jnp.float32),
            pltpu.VMEM((group, 2, edge, edge), jnp.float32),
            pltpu.VMEM((2 * edge, 2 * edge), jnp.bfloat16),
            pltpu.VMEM((2 * edge, 2 * edge), jnp.bfloat16),
            pltpu.SMEM(positions.shape[1:], jnp.int32),
            pltpu.SemaphoreType.DMA,
        ],
        compiler_params=pltpu.CompilerParams(vmem_limit_bytes=VMEM_LIMIT),
    )(
        positions[0],
        *[piece for piece, _ in pieces],
        illumination,
        amplitudes[0],
        dft_table(edge),
    )
    imag_outs, real_outs = outs[:tile_count], outs[tile_count:]

    imag_part, real_part = (
        add_up(part[0], *[swap(part[k], "tile", k) for k in range(1, tile_count)]).astype(jnp.bfloat16)
        for part in (imag_outs, real_outs)
    )
    imag_sum = add_up(imag_part[0], *[swap(imag_part[j], "cuts", j) for j in range(1, cuts_count)])[None]
    own_real = add_up(real_part[0], *[swap(real_part[j], "cuts", j) for j in range(1, cuts_count)])
    share = jnp.stack([own_real, imag_sum[0]])
    new_objects = objects + share[None]
    phase = (object_half[1].astype(jnp.float32) + imag_sum).astype(jnp.bfloat16)
    own_phase = phase[0]
    rows = [own_phase]
    for j in range(1, cuts_count):
        rows.append(swap(own_phase, "cuts", j))
    phase = jnp.stack(rows)
    others = [swap(phase, "angle", a) for a in range(1, angle_count)]
    volume_rows = cuts_count * band_rows

    def product(masks, blocks, *before):
        return pl.pallas_call(
            functools.partial(volume_kernel, masks, cuts_count),
            out_shape=jax.ShapeDtypeStruct((volume_rows, voxel_count), jnp.float32),
            in_specs=[vmem] * (len(blocks) + len(before) + 1),
            out_specs=vmem,
            scratch_shapes=[pltpu.VMEM((len(masks), volume_rows, image_width), jnp.bfloat16)],
            compiler_params=pltpu.CompilerParams(vmem_limit_bytes=VMEM_LIMIT),
        )(*blocks, *before, projector)

    volume = product((0,), (phase,))
    if angle_count > 1:
        volume = product(tuple(range(1, angle_count)), others, volume)
    return new_objects, volume


def solution(mesh):
    in_specs = (
        P("angle", None, ("tile", "cuts"), None),
        P(),
        P("angle", ("tile", "cuts"), None),
        P("angle", ("tile", "cuts"), None, None),
        P(None, ("angle", "cuts")),
    )
    out_specs = (P("angle", None, ("tile", "cuts"), None), P("tile", ("angle", "cuts")))
    return jax.shard_map(compute, mesh=mesh, in_specs=in_specs, out_specs=out_specs, check_vma=False)
```

```python
import functools

import jax
import jax.numpy as jnp
import numpy as np
from jax import lax
from jax.experimental import pallas as pl
from jax.experimental.pallas import tpu as pltpu
from jax.sharding import PartitionSpec as P


step_size = 0.1
LANES = 128
GROUP = 16
VMEM_LIMIT = 24 * 2**20


def dft_table(width):
    index = np.arange(width)
    phase = (index[:, None] * index[None, :] % width) * (2.0 * np.pi / width)
    real = np.cos(phase) / np.sqrt(width)
    imag = -np.sin(phase) / np.sqrt(width)
    return jnp.asarray(np.stack([real, imag]).astype(jnp.bfloat16))


def dot(a, b):
    return jnp.dot(a, b, preferred_element_type=jnp.float32)


def patch_kernel(
    layout,
    place_ref,
    *refs,
):
    (in_ids, out_ids, band_rows, _, cuts_count, group) = layout
    n_in, n_out = len(in_ids), len(out_ids)
    piece_refs = refs[:n_in]
    probe_ref, amp_ref, table_ref = refs[n_in : n_in + 3]
    out_refs = refs[n_in + 3 : n_in + 3 + n_out]
    image, canvas, exits, right_ref, left_ref, places, place_sem = refs[n_in + 3 + n_out :]
    fetch = pltpu.make_async_copy(place_ref, places, place_sem)
    fetch.start()
    col_tiles = image.shape[1]
    edge = probe_ref.shape[-1]
    patches = amp_ref.shape[0]
    tile_at, cuts_at = lax.axis_index("tile"), lax.axis_index("cuts")

    def band_start(k, j):
        band = (tile_at ^ k) * cuts_count + (cuts_at ^ j)
        return pl.multiple_of(band * band_rows, band_rows)

    for ref, spots in zip(piece_refs, in_ids):
        for slot, (k, j) in enumerate(spots):
            rows = pl.ds(band_start(k, j), band_rows)
            for plane in range(2):
                for col in range(col_tiles):
                    image[plane, col, rows, :] = ref[
                        slot, plane, :, col * LANES : (col + 1) * LANES
                    ].astype(jnp.float32)
    canvas[...] = jnp.zeros_like(canvas)
    for top in range(2):
        for side in range(2):
            block = table_ref[top ^ side]
            here = (slice(top * edge, (top + 1) * edge), slice(side * edge, (side + 1) * edge))
            right_ref[here] = -block if top > side else block
            left_ref[here] = -block if top < side else block
    lane = lax.broadcasted_iota(jnp.int32, (edge, LANES), 1)

    def several(step, carry):
        spots = []
        for q in range(group):
            row_at = places[group * step + q, 0]
            col_at = places[group * step + q, 1]
            col = jnp.minimum(lax.div(col_at, LANES), col_tiles - 2)
            spots.append((pl.ds(row_at, edge), col, col_at - col * LANES))
        probe_real, probe_imag = probe_ref[0], probe_ref[1]
        stacked = []
        for q, (rows, col, shift) in enumerate(spots):
            back = (LANES - shift) & (LANES - 1)
            window = []
            for plane in range(2):
                near = image[plane, col, rows, :]
                far = image[plane, col + 1, rows, :]
                window.append(pltpu.roll(jnp.where(lane < shift, far, near), back, 1))
            exit_real = probe_real * window[0] - probe_imag * window[1]
            exit_imag = probe_real * window[1] + probe_imag * window[0]
            exits[q, 0] = exit_real
            exits[q, 1] = exit_imag
            stacked.append(jnp.concatenate([exit_real, exit_imag], 1).astype(jnp.bfloat16))
        spread = dot(jnp.concatenate(stacked, 0), right_ref[...]).astype(jnp.bfloat16)

        def side_by_side(x):
            halves = [
                jnp.concatenate(
                    [x[q * edge : (q + 1) * edge, h * edge : (h + 1) * edge] for q in range(group)], 1
                )
                for h in range(2)
            ]
            return jnp.concatenate(halves, 0)

        spectrum = dot(left_ref[...], side_by_side(spread))
        real, imag = spectrum[:edge], spectrum[edge:]
        amp = jnp.concatenate([amp_ref[group * step + q] for q in range(group)], 1)
        scale = amp.astype(jnp.float32) * lax.rsqrt(jnp.maximum(real * real + imag * imag, 1.0))
        real = (real * scale).astype(jnp.bfloat16)
        imag = (imag * scale).astype(jnp.bfloat16)
        projected = jnp.concatenate(
            [
                jnp.concatenate([part[:, q * edge : (q + 1) * edge] for part in (real, imag)], 1)
                for q in range(group)
            ],
            0,
        )
        back_half = dot(projected, left_ref[...]).astype(jnp.bfloat16)
        revised = dot(right_ref[...], side_by_side(back_half))
        for q, (rows, col, shift) in enumerate(spots):
            diff_real = revised[:edge, q * edge : (q + 1) * edge] - exits[q, 0]
            diff_imag = revised[edge:, q * edge : (q + 1) * edge] - exits[q, 1]
            terms = (
                step_size * (probe_real * diff_real + probe_imag * diff_imag),
                step_size * (probe_real * diff_imag - probe_imag * diff_real),
            )
            for plane in range(2):
                moved = pltpu.roll(terms[plane], shift & (LANES - 1), 1)
                near = canvas[plane, col, rows, :] + jnp.where(lane >= shift, moved, 0.0)
                far = canvas[plane, col + 1, rows, :] + jnp.where(lane < shift, moved, 0.0)
                canvas[plane, col, rows, :] = near
                canvas[plane, col + 1, rows, :] = far
        return carry

    fetch.wait()
    lax.fori_loop(0, patches // group, several, 0)
    for ref, (plane, k) in zip(out_refs, out_ids):
        for j in range(cuts_count):
            rows = pl.ds(band_start(k, j), band_rows)
            for col in range(col_tiles):
                ref[j, :, col * LANES : (col + 1) * LANES] = canvas[plane, col, rows, :].astype(
                    jnp.bfloat16
                )


def volume_kernel(masks, cuts_count, *refs):
    phase_refs = refs[: len(masks)]
    weight_ref, out_ref, rows_ref = refs[-3:]
    cuts_at, angle_at = lax.axis_index("cuts"), lax.axis_index("angle")
    band_rows, width = phase_refs[0].shape[1:]
    total = refs[len(masks)][...] if len(refs) > len(masks) + 3 else None
    for a, (mask, ref) in enumerate(zip(masks, phase_refs)):
        for j in range(cuts_count):
            rows = pl.ds(pl.multiple_of((cuts_at ^ j) * band_rows, band_rows), band_rows)
            rows_ref[a, rows, :] = ref[j]
        weight = weight_ref[pl.ds(pl.multiple_of((angle_at ^ mask) * width, width), width), :]
        part = dot(rows_ref[a], weight)
        total = part if total is None else total + part
    out_ref[...] = total


def swap(x, axis, mask):
    size = lax.axis_size(axis)
    return lax.ppermute(x, axis, [(i, i ^ mask) for i in range(size)])


def add_up(*terms):
    total = terms[0].astype(jnp.float32)
    for term in terms[1:]:
        total = total + term.astype(jnp.float32)
    return total


def compute(objects, illumination, positions, amplitudes, projector):
    cuts_count = lax.axis_size("cuts")
    tile_count = lax.axis_size("tile")
    angle_count = lax.axis_size("angle")
    band_rows, image_width = objects.shape[2:]
    edge = illumination.shape[-1]
    image_rows = band_rows * tile_count * cuts_count
    voxel_count = projector.shape[1]
    object_half = objects[0].astype(jnp.bfloat16)

    near = [object_half]
    for j in range(1, cuts_count):
        near.append(swap(object_half, "cuts", j))
    own_spread = []
    for k in range(1, tile_count):
        own_spread.append(swap(object_half, "tile", k))
    far = jnp.stack(near[1:])
    pieces = [(object_half[None], ((0, 0),)), (far, tuple((0, j) for j in range(1, cuts_count)))]
    pieces += [(own_spread[k - 1][None], ((k, 0),)) for k in range(1, tile_count)]
    for k in range(1, tile_count):
        pieces.append((swap(far, "tile", k), tuple((k, j) for j in range(1, cuts_count))))

    out_ids = tuple((plane, k) for plane in (1, 0) for k in range(tile_count))
    group = next(g for g in (GROUP, 8, 4, 2, 1) if amplitudes.shape[1] % g == 0)
    layout = (tuple(ids for _, ids in pieces), out_ids, band_rows, tile_count, cuts_count, group)
    vmem = pl.BlockSpec(memory_space=pltpu.VMEM)
    smem = pl.BlockSpec(memory_space=pltpu.SMEM)
    col_tiles = image_width // LANES
    outs = pl.pallas_call(
        functools.partial(patch_kernel, layout),
        out_shape=[
            jax.ShapeDtypeStruct((cuts_count, band_rows, image_width), jnp.bfloat16)
            for _ in out_ids
        ],
        in_specs=[pl.BlockSpec(memory_space=pl.ANY)] + [vmem] * (len(pieces) + 3),
        out_specs=[vmem] * len(out_ids),
        scratch_shapes=[
            pltpu.VMEM((2, col_tiles, image_rows, LANES), jnp.float32),
            pltpu.VMEM((2, col_tiles, image_rows, LANES), jnp.float32),
            pltpu.VMEM((group, 2, edge, edge), jnp.float32),
            pltpu.VMEM((2 * edge, 2 * edge), jnp.bfloat16),
            pltpu.VMEM((2 * edge, 2 * edge), jnp.bfloat16),
            pltpu.SMEM(positions.shape[1:], jnp.int32),
            pltpu.SemaphoreType.DMA,
        ],
        compiler_params=pltpu.CompilerParams(vmem_limit_bytes=VMEM_LIMIT),
    )(
        positions[0],
        *[piece for piece, _ in pieces],
        illumination,
        amplitudes[0],
        dft_table(edge),
    )
    imag_outs, real_outs = outs[:tile_count], outs[tile_count:]

    def spread_sum(terms, axis):
        got = []
        for step in range(1, len(terms)):
            got.append(swap(terms[step], axis, step))
        return add_up(terms[0], *got)

    if angle_count > 1:
        token = swap(imag_outs[0][0, :8, :LANES], "angle", 1)
        anywhere = pl.BlockSpec(memory_space=pl.ANY)
        going = pl.pallas_call(
            lambda *refs: None,
            out_shape=[jax.ShapeDtypeStruct(x.shape, x.dtype) for x in real_outs[1:]],
            in_specs=[anywhere] * tile_count,
            out_specs=[anywhere] * (tile_count - 1),
            input_output_aliases={i: i for i in range(tile_count - 1)},
            compiler_params=pltpu.CompilerParams(vmem_limit_bytes=2**20),
        )(*real_outs[1:], token)
        real_outs = [real_outs[0]] + list(going)
    imag_part = spread_sum(imag_outs, "tile").astype(jnp.bfloat16)
    real_part = spread_sum(list(real_outs), "tile").astype(jnp.bfloat16)
    imag_sum = spread_sum(imag_part, "cuts")[None]
    own_real = spread_sum(real_part, "cuts")
    share = jnp.stack([own_real, imag_sum[0]])
    new_objects = objects + share[None]
    phase = (object_half[1].astype(jnp.float32) + imag_sum).astype(jnp.bfloat16)
    own_phase = phase[0]
    rows = [own_phase]
    for j in range(1, cuts_count):
        rows.append(swap(own_phase, "cuts", j))
    phase = jnp.stack(rows)
    others = [swap(phase, "angle", a) for a in range(1, angle_count)]
    volume_rows = cuts_count * band_rows

    def product(masks, blocks, *before):
        return pl.pallas_call(
            functools.partial(volume_kernel, masks, cuts_count),
            out_shape=jax.ShapeDtypeStruct((volume_rows, voxel_count), jnp.float32),
            in_specs=[vmem] * (len(blocks) + len(before) + 1),
            out_specs=vmem,
            scratch_shapes=[pltpu.VMEM((len(masks), volume_rows, image_width), jnp.bfloat16)],
            compiler_params=pltpu.CompilerParams(vmem_limit_bytes=VMEM_LIMIT),
        )(*blocks, *before, projector)

    volume = product((0,), (phase,))
    if angle_count > 1:
        volume = product(tuple(range(1, angle_count)), others, volume)
    return new_objects, volume


def solution(mesh):
    in_specs = (
        P("angle", None, ("tile", "cuts"), None),
        P(),
        P("angle", ("tile", "cuts"), None),
        P("angle", ("tile", "cuts"), None, None),
        P(None, ("angle", "cuts")),
    )
    out_specs = (P("angle", None, ("tile", "cuts"), None), P("tile", ("angle", "cuts")))
    return jax.shard_map(compute, mesh=mesh, in_specs=in_specs, out_specs=out_specs, check_vma=False)
```
